32 devices in a mesh: mem: 16 (over z, x, core), gy: 2 (over y).
Axes of the slice: x: 2, y: 2, z: 4, core: 2. Of those that a mesh axis runs over, the one named last changes fastest.
Arguments:
- state: bfloat16 [64, 2, 512, 256], P('mem', None, None, 'gy'), may hold values from -6 to 6
- obs_index: int32 [16, 2, 256], P('mem', 'gy'), may hold values from 0 to 8191
- obs_count: int32 [16, 2], P('mem', 'gy'), may hold values from 1 to 256, as said below
- obs_value: float32 [16, 2, 256], P('mem', 'gy'), may hold values from -6 to 6
- obs_var: float32 [16, 2, 256], P('mem', 'gy'), may hold values from 0.1 to 1
- radius: int32 [16, 2], P('mem', 'gy'), may hold values from 8 to 16
Outputs:
- analysis: bfloat16 [64, 2, 512, 256], P('mem', None, None, 'gy')
The draws below stay inside these ranges and needn't reach their ends.
Inputs may be any that keep to these rules, and one draw needn't show every extreme that they name: `obs_count`: Tiles' counts are skewed: most tiles have few live slots, some many, and in every draw some tile has all 256 slots live.
All inputs are finite; a program needn't handle non-finite values.
Results may differ from the reference program's by a relative error of at most 0.0028.
The reference program's roundings to bfloat16 on the way (of `mixing`) count: a program that leaves them out, or rounds other values in their place, can miss the bound.
Values may be sent and summed in bfloat16 or wider, within the bound.
No kernel may reach another device: no remote copies, remote signals or barrier semaphores. Data moves between devices by JAX's collectives and lax.ppermute only.
A program may use at most 64 MiB of HBM per device.

```python
import math
import jax
import jax.numpy as jnp
from jax import lax

K = 64
LEV = 2
ROWS = 128
COLS = 32
BLK = 16
OBS = 256
RMAX = 16
NSI = 10
TILES_X = 16
TILES_Y = 2
NXG = 512
NYG = 256
N_MEM = 16
N_GY = 2


def draw_obs_count(key, part):
    key_light = jax.random.fold_in(key, 11)
    key_heavy = jax.random.fold_in(key, 12)
    key_pick = jax.random.fold_in(key, 13)
    key_spot = jax.random.fold_in(key, 14)
    grid_shape = (TILES_X, TILES_Y)
    light = jax.random.randint(key_light, grid_shape, 1, OBS // 4 + 1)
    heavy = jax.random.randint(key_heavy, grid_shape, OBS // 2, OBS + 1)
    chosen = jax.random.randint(key_pick, grid_shape, 0, 4) == 0
    counts = jnp.where(chosen, heavy, light).reshape(-1)
    spot = jax.random.randint(key_spot, (), 0, TILES_X * TILES_Y)
    counts = jnp.where(jnp.arange(TILES_X * TILES_Y) == spot, OBS, counts)
    return counts.reshape(grid_shape).astype(jnp.int32)


def touch_ends(values, rng, least, top_value):
    extent = values.shape
    place = [jax.random.randint(jax.random.fold_in(rng, axis), (), 0, extent[axis]) for axis in range(len(extent))]
    values = values.at[tuple(place)].set(least)
    longest = extent.index(max(extent))
    place[longest] = (place[longest] + 1) % extent[longest]
    return values.at[tuple(place)].set(top_value)


def level_of(key, shape, pieces, smallest, largest):
    def one(axis_at, blocks):
        heights = jax.random.uniform(jax.random.fold_in(jax.random.fold_in(key, 6), axis_at), (blocks,), jnp.float32, smallest / len(pieces), largest / len(pieces))
        return jnp.repeat(jnp.exp(heights), shape[axis_at] // blocks).reshape((-1,) + (1,) * (len(shape) - axis_at - 1))

    level = one(*pieces[0])
    for cut in pieces[1:]:
        level = level * one(*cut)
    return level


def centred(key, extent, scale, bound, cuts=(), kind=jnp.bfloat16):
    level = level_of(key, extent, cuts, -0.22, 0.18) if cuts else 1.0
    entries = jax.random.normal(key, extent, jnp.float32) * scale * level
    return jnp.minimum(jnp.maximum(entries, -bound), bound).astype(kind)


def setup_inputs(seed: int = 0) -> dict:
    key_of = jax.random.split(jax.random.key(seed), 7)
    state = centred(key_of[0], (K, LEV, NXG, NYG), 1.0, 6.0, ((0, 16), (3, 2)))
    obs_index = touch_ends(jax.random.randint(key_of[1], (TILES_X, TILES_Y, OBS), 0, LEV * COLS * ROWS), jax.random.fold_in(key_of[1], 1), 0, (LEV * COLS * ROWS) - 1).astype(jnp.int32)
    obs_count = draw_obs_count(jax.random.fold_in(key_of[6], 71), 0)
    obs_value = centred(key_of[3], (TILES_X, TILES_Y, OBS), 1.0, 6.0, ((0, 16), (1, 2)), jnp.float32)
    obs_var = jnp.clip(jnp.exp(math.log(1.0) - 2.3025851 * jax.random.uniform(key_of[4], (TILES_X, TILES_Y, OBS), jnp.float32) ** level_of(key_of[4], (TILES_X, TILES_Y, OBS), ((0, 16), (1, 2)), -0.2, 0.2)), 0.1, 1.0)
    radius = touch_ends(jax.random.randint(key_of[5], (TILES_X, TILES_Y), RMAX // 2, RMAX + 1), jax.random.fold_in(key_of[5], 1), RMAX // 2, RMAX).astype(jnp.int32)
    return dict(state=state, obs_index=obs_index, obs_count=obs_count, obs_value=obs_value, obs_var=obs_var, radius=radius)


highest = lax.Precision.HIGHEST

def build_payload(ensemble, obs_slots, live_count, observed, variance):
    slot_total = obs_slots.shape[0]
    centre = lax.optimization_barrier(jnp.mean(ensemble, axis=0))
    spread = ensemble - centre
    is_live = jnp.arange(slot_total, dtype=jnp.int32) < live_count
    weight = jnp.where(is_live, 1.0 / variance, jnp.zeros_like(variance))
    innovation = observed - centre
    col_pos = (obs_slots // ROWS % COLS).astype(ensemble.dtype)
    row_pos = (obs_slots % ROWS).astype(ensemble.dtype)
    return jnp.concatenate([spread, innovation[None], weight[None], col_pos[None], row_pos[None]], axis=0)

def transforms(nearby, radius):
    dtype = nearby.dtype
    count_c = COLS // BLK
    count_r = ROWS // BLK
    block_ids = jnp.arange(count_c * count_r, dtype=jnp.int32)
    centre_c = (block_ids // count_r * BLK).astype(dtype) + (BLK - 1) / 2.0
    centre_r = (block_ids % count_r * BLK).astype(dtype) + (BLK - 1) / 2.0
    reach_sq = jnp.square(radius[0].astype(dtype))
    gram_sum = jnp.zeros((count_c * count_r, K, K), dtype)
    drive_sum = jnp.zeros((count_c * count_r, K), dtype)
    for step_x in range(3):
        for step_y in range(3):
            neighbour = nearby[step_x, step_y]
            spread = neighbour[:K]
            innovation = neighbour[K]
            weight = neighbour[K + 1]
            gap_c = (step_x - 1) * COLS + neighbour[K + 2][None, :] - centre_c[:, None]
            gap_r = (step_y - 1) * ROWS + neighbour[K + 3][None, :] - centre_r[:, None]
            taper_val = jnp.square(jnp.maximum(1.0 - (gap_c * gap_c + gap_r * gap_r) / reach_sq, 0.0))
            local_weight = taper_val * weight[None, :]
            weighted = local_weight[:, None, :] * spread[None]
            gram_sum = gram_sum + jnp.einsum('bko,jo->bkj', weighted, spread, precision=highest)
            drive_sum = drive_sum + jnp.einsum('bko,o->bk', weighted, innovation, precision=highest)
    identity = jnp.eye(K, dtype=dtype)
    system = (K - 1.0) * identity + gram_sum
    trace_scale = jnp.trace(system, axis1=1, axis2=2)
    upper_iter = system / trace_scale[:, None, None]
    lower_iter = jnp.broadcast_to(identity, system.shape)
    for sweep in range(NSI):
        factor = 1.5 * identity - 0.5 * jnp.einsum('bij,bjk->bik', lower_iter, upper_iter, precision=highest)
        upper_iter = jnp.einsum('bij,bjk->bik', upper_iter, factor, precision=highest)
        lower_iter = jnp.einsum('bij,bjk->bik', factor, lower_iter, precision=highest)
    inv_root = lower_iter / jnp.sqrt(trace_scale)[:, None, None]
    posterior = jnp.einsum('bij,bjk->bik', inv_root, inv_root, precision=highest)
    mean_shift = jnp.einsum('bkj,bj->bk', posterior, drive_sum, precision=highest)
    transform = jnp.sqrt(K - 1.0) * inv_root + mean_shift[:, :, None]
    mixing = 1.0 / K + transform - lax.optimization_barrier(jnp.mean(transform, axis=1, keepdims=True))
    return mixing.astype(jnp.bfloat16)

def mix_tile(tile_state, mixing):
    count_c = COLS // BLK
    count_r = ROWS // BLK
    blocks = tile_state.reshape(K, LEV, count_c, BLK, count_r, BLK).astype(jnp.float32)
    mix_table = mixing.reshape(count_c, count_r, K, K).astype(jnp.float32)
    mixed_tile = jnp.einsum('abkm,klaibj->mlaibj', mix_table, blocks)
    return mixed_tile.reshape(K, LEV, COLS, ROWS).astype(jnp.bfloat16)

def reference(state, obs_index, obs_count, obs_value, obs_var, radius):
    tiles_x = N_MEM
    tiles_y = N_GY
    anchor = jnp.zeros((), jnp.int32)

    def tile_at(tile_x, tile_y):
        return lax.dynamic_slice(state, (anchor, anchor, (tile_x * COLS).astype(jnp.int32), (tile_y * ROWS).astype(jnp.int32)), (K, LEV, COLS, ROWS))

    def payload_of(flat_id):
        tile_x = flat_id // tiles_y
        tile_y = flat_id % tiles_y
        tile_state = tile_at(tile_x, tile_y)
        obs_slots = obs_index[tile_x, tile_y]
        ensemble = jnp.take(tile_state.reshape(K, LEV * COLS * ROWS), obs_slots, axis=1).astype(jnp.float32)
        return build_payload(ensemble, obs_slots, obs_count[tile_x, tile_y], obs_value[tile_x, tile_y], obs_var[tile_x, tile_y])
    tile_ids = jnp.arange(tiles_x * tiles_y, dtype=jnp.int32)
    payloads = lax.map(payload_of, tile_ids).reshape(tiles_x, tiles_y, K + 4, OBS)
    padded = jnp.pad(payloads, ((1, 1), (1, 1), (0, 0), (0, 0)))

    def analyse(flat_id):
        tile_x = flat_id // tiles_y
        tile_y = flat_id % tiles_y
        nearby = lax.dynamic_slice(padded, (tile_x, tile_y, anchor, anchor), (3, 3, K + 4, OBS))
        return mix_tile(tile_at(tile_x, tile_y), transforms(nearby, radius[tile_x, tile_y][None]))
    result = lax.map(analyse, tile_ids)
    result = result.reshape(tiles_x, tiles_y, K, LEV, COLS, ROWS).transpose(2, 3, 0, 4, 1, 5)
    return result.reshape(K, LEV, tiles_x * COLS, tiles_y * ROWS)
```

```python
import functools
import math

import jax
import jax.numpy as jnp
from jax import lax
from jax.experimental import pallas as pl
from jax.experimental.pallas import tpu as pltpu
from jax.sharding import PartitionSpec as P

BLK = 16
NSI = 10
f32 = jnp.float32
bf16 = jnp.bfloat16
META = 8


def dot(a, b):
    return lax.dot_general(a, b, (((1,), (0,)), ((), ())), preferred_element_type=f32)


def dot_t(a, b):
    return lax.dot_general(a, b, (((1,), (1,)), ((), ())), preferred_element_type=f32)


def split3(x):
    high = x.astype(bf16)
    rest = x - high.astype(f32)
    mid = rest.astype(bf16)
    low = (rest - mid.astype(f32)).astype(bf16)
    return high, mid, low


def gather_kernel(x_ref, idx_ref, ens_ref):
    members, cells, rows = x_ref.shape
    slots = idx_ref.shape[1]
    idx = idx_ref[...]
    row = lax.rem(idx, rows)
    cell = lax.div(idx, rows)
    pick_row = jnp.where(lax.broadcasted_iota(jnp.int32, (rows, slots), 0) == row, 1.0, 0.0).astype(bf16)
    pick_cell = lax.broadcasted_iota(jnp.int32, (cells, slots), 0) == cell
    for first in range(0, members, 8):
        x = x_ref[first : first + 8].reshape(8 * cells, rows)
        found = dot(x, pick_row).reshape(8, cells, slots)
        ens_ref[first : first + 8, :] = jnp.sum(jnp.where(pick_cell[None], found, 0.0), axis=1)


def gather_call(x, obs_slots):
    members, cells, rows = x.shape
    slots = obs_slots.shape[0]
    group = min(members, 16)
    return pl.pallas_call(
        gather_kernel,
        grid=(members // group,),
        in_specs=[
            pl.BlockSpec((group, cells, rows), lambda i: (i, 0, 0)),
            pl.BlockSpec((1, slots), lambda i: (0, 0)),
        ],
        out_specs=pl.BlockSpec((group, slots), lambda i: (i, 0)),
        out_shape=jax.ShapeDtypeStruct((members, slots), f32),
        name="gather",
    )(x, obs_slots[None])


def recursion_product(a, b, left):
    ah, am, al = a
    bh, bm, bl = b
    return dot(
        jnp.concatenate([ah, am, jnp.where(left, al, ah)], axis=1),
        jnp.concatenate([bh, bm, bh, bm, bh, bl], axis=0),
    )


def transform_kernel(num_y, counts, scal_ref, *refs):
    count_c, count_r, cols, rows = counts
    ens_refs = refs[: 3 * num_y]
    meta_refs = refs[3 * num_y : 4 * num_y]
    out_ref, lhs_ref, gram_ref, up_ref, low_ref = refs[4 * num_y :]
    members, slots = ens_refs[0].shape
    wide = 2 * members
    odd_x = scal_ref[0] == 1
    odd_y = scal_ref[1] == 1
    reach = scal_ref[2].astype(f32)
    reach_sq = reach * reach

    def tile(y, which):
        own, pair, other = ens_refs[3 * y : 3 * y + 3]
        if which == 0:
            return own[...].astype(f32), meta_refs[y][0]
        pair_first = odd_x if which < 0 else jnp.logical_not(odd_x)
        ens = jnp.where(pair_first, pair[...].astype(f32), other[...].astype(f32))
        meta = jnp.where(pair_first, meta_refs[y][1], meta_refs[y][2])
        return ens, meta

    def prepare(y, which):
        ens, meta = tile(y, which)
        centre = jnp.sum(ens, axis=0, keepdims=True) * (1.0 / members)
        spread = ens - centre
        innovation = meta[0:1] - centre
        sh, sm, sl = split3(spread)
        line = lax.broadcasted_iota(jnp.int32, (members, slots), 0)
        ih, im, il = (part.astype(f32) for part in split3(innovation))
        extra = jnp.where(line == 0, ih, jnp.where(line == 1, im, jnp.where(line == 2, il, 0.0))).astype(bf16)
        return spread, meta, jnp.concatenate([sh, sm, sl, extra], axis=0)

    def local_weight(meta, dx, dy, block_c, block_r):
        gap_c = dx * cols + meta[2:3] - (block_c * float(BLK) + (BLK - 1) / 2.0)
        gap_r = dy * float(rows) + meta[3:4] - (block_r * float(BLK) + (BLK - 1) / 2.0)
        taper = jnp.maximum(1.0 - (gap_c * gap_c + gap_r * gap_r) / reach_sq, 0.0)
        return taper * taper * meta[1:2]

    def put(part, total, column, rho, spread):
        weighted = rho * spread
        for level, piece in enumerate(split3(weighted)):
            start = level * total + part * members
            lhs_ref[start : start + members, column : column + slots] = piece

    own_tiles = [prepare(y, 0) for y in range(num_y)]
    lines = lax.broadcasted_iota(jnp.int32, (count_r, slots), 0).astype(f32)
    for a in range(count_c):
        sides = [0] + ([-1] if a == 0 else []) + ([1] if a == count_c - 1 else [])
        tiles = [[own_tiles[y] if side == 0 else prepare(y, side) for side in sides] for y in range(num_y)]
        total = count_r * members
        for at, (side, (spread, meta, rhs)) in enumerate(zip(sides, tiles[0])):
            rho = local_weight(meta, float(side), 0.0, float(a), lines)
            for r in range(count_r):
                put(r, total, at * slots, rho[r : r + 1], spread)
        width = len(sides) * slots
        rhs = jnp.concatenate([t[2] for t in tiles[0]], axis=1)
        found = dot_t(lhs_ref[: 3 * total, :width], rhs)
        found = found[:total] + found[total : 2 * total] + found[2 * total :]
        gram_ref[a * count_r : (a + 1) * count_r] = found.reshape(count_r, members, 4 * members)
        for y in range(1, num_y):
            above = jnp.logical_not(odd_y) if y == 1 else odd_y
            dy = jnp.where(above, 1.0, -1.0)
            edge = jnp.where(above, count_r - 1, 0)
            for at, (side, (spread, meta, rhs)) in enumerate(zip(sides, tiles[y])):
                rho = local_weight(meta, float(side), dy, float(a), edge.astype(f32))
                put(0, members, at * slots, rho, spread)
            rhs = jnp.concatenate([t[2] for t in tiles[y]], axis=1)
            found = dot_t(lhs_ref[: 3 * members, :width], rhs)
            found = found[:members] + found[members : 2 * members] + found[2 * members :]
            gram_ref[a * count_r + edge] += found

    blocks = count_c * count_r
    line = lax.broadcasted_iota(jnp.int32, (members, wide), 0)
    lane = lax.broadcasted_iota(jnp.int32, (members, wide), 1)
    left = lane < members
    half = jnp.where(lane == line, 1.0, 0.0)
    eye = jnp.where(lane == line + members, 1.0, half)

    def keep(ref, b, value):
        for part, piece in enumerate(split3(value)):
            ref[b, part] = piece

    def held(ref, b):
        return ref[b, 0], ref[b, 1], ref[b, 2]

    scales = []
    drives = []
    starts = []
    for b in range(blocks):
        found = gram_ref[b]
        high, tail = found[:, :wide], found[:, wide:]
        once = high + jnp.where(left, tail, 0.0)
        system = (members - 1.0) * eye + once + pltpu.roll(once, members, 1)
        drive = jnp.sum(jnp.where(left, 0.0, tail), axis=1, keepdims=True)
        drives.append(jnp.sum(drive * eye, axis=0, keepdims=True))
        scale = jnp.sum(jnp.sum(system * half, axis=1, keepdims=True), axis=0, keepdims=True)
        scales.append(scale)
        starts.append(system / scale)
    for b in range(blocks):
        factor = 1.5 * eye - 0.5 * starts[b]
        keep(low_ref, b, factor)
        keep(up_ref, b, recursion_product(split3(starts[b]), split3(factor), left))

    def sweep(_, carry):
        factors = []
        for b in range(blocks):
            product = recursion_product(held(low_ref, b), held(up_ref, b), left)
            factors.append(split3(1.5 * eye - 0.5 * product))
        for b in range(blocks):
            upper = recursion_product(held(up_ref, b), factors[b], left)
            lower = recursion_product(factors[b], held(low_ref, b), left)
            keep(up_ref, b, upper)
            keep(low_ref, b, lower)
        return carry

    lax.fori_loop(0, NSI - 1, sweep, 0)

    mixed = []
    for b in range(blocks):
        lh, lm, ll = held(low_ref, b)
        lower = lh.astype(f32) + lm.astype(f32) + ll.astype(f32)
        inv_root = lower * lax.rsqrt(scales[b])
        first = jnp.sum(jnp.where(left, inv_root * drives[b], 0.0), axis=1, keepdims=True)
        shift = jnp.sum(inv_root * first, axis=0, keepdims=True)
        transform = math.sqrt(members - 1.0) * inv_root + shift
        mean = jnp.sum(jnp.where(left, transform, 0.0), axis=1, keepdims=True) * (1.0 / members)
        mixed.append(1.0 / members + transform - mean)
    for a in range(count_c):
        for r in range(0, count_r, 2):
            b = a * count_r + r
            both = jnp.where(left, mixed[b], mixed[b + 1])
            out_ref[a, :, r * members : (r + 2) * members] = both.astype(bf16)


def transform_call(scalars, ens, meta, cols, rows):
    num_y = len(meta)
    members, slots = ens[0].shape
    count_c, count_r = cols // BLK, rows // BLK
    blocks = count_c * count_r
    vmem = pl.BlockSpec(memory_space=pltpu.VMEM)
    return pl.pallas_call(
        functools.partial(transform_kernel, num_y, (count_c, count_r, cols, rows)),
        in_specs=[pl.BlockSpec(memory_space=pltpu.SMEM)] + [vmem] * (4 * num_y),
        out_specs=vmem,
        out_shape=jax.ShapeDtypeStruct((count_c, members, count_r * members), bf16),
        scratch_shapes=[
            pltpu.VMEM((3 * count_r * members, 2 * slots), bf16),
            pltpu.VMEM((blocks, members, 4 * members), f32),
            pltpu.VMEM((blocks, 3, members, 2 * members), bf16),
            pltpu.VMEM((blocks, 3, members, 2 * members), bf16),
        ],
        name="transform",
    )(scalars, *ens, *meta)


def mix_kernel(count_c, count_r, cols, mix_ref, x_ref, out_ref, in32_ref, out32_ref):
    members, cells, rows = x_ref.shape
    for k in range(0, members, 8):
        in32_ref[k * cells : (k + 8) * cells] = x_ref[k : k + 8].reshape(8 * cells, rows).astype(f32)
    lane_block = lax.broadcasted_iota(jnp.int32, (members, rows), 1) // BLK
    masks = [(lane_block == r) for r in range(count_r)]
    zero = jnp.zeros((members, rows), bf16)
    for cell in range(0, cells, 2):
        a = (cell % cols) // BLK
        pieces = []
        for one in (cell, cell + 1):
            x = in32_ref[pl.ds(one, members, stride=cells), :].astype(bf16)
            pieces.append(jnp.concatenate([jnp.where(mask, x, zero) for mask in masks], axis=0))
        found = dot(mix_ref[a], jnp.concatenate(pieces, axis=1))
        for at in range(2):
            out32_ref[pl.ds(cell + at, members, stride=cells), :] = found[:, at * rows : (at + 1) * rows]
    for k in range(0, members, 8):
        out_ref[k : k + 8] = out32_ref[k * cells : (k + 8) * cells].astype(bf16).reshape(8, cells, rows)


def mix_call(mixing, x, cols):
    members, cells, rows = x.shape
    count_c, count_r = cols // BLK, rows // BLK
    vmem = pl.BlockSpec(memory_space=pltpu.VMEM)
    return pl.pallas_call(
        functools.partial(mix_kernel, count_c, count_r, cols),
        in_specs=[vmem, vmem],
        out_specs=vmem,
        out_shape=jax.ShapeDtypeStruct(x.shape, bf16),
        scratch_shapes=[pltpu.VMEM((members * cells, rows), f32)] * 2,
        name="mix",
    )(mixing, x)


def swap_pairs(count, first):
    pairs = []
    for i in range(first, count - 1, 2):
        pairs += [(i, i + 1), (i + 1, i)]
    return pairs


def local(state, obs_index, obs_count, obs_value, obs_var, radius):
    n_x = lax.axis_size("mem")
    n_y = lax.axis_size("gy")
    held, levels, all_cols, rows = state.shape
    cols = all_cols // n_x
    members = held * n_x
    obs_slots = obs_index[0, 0]
    slots = obs_slots.shape[0]

    def swap_x(value, first):
        return lax.ppermute(value, "mem", swap_pairs(n_x, first))

    def swap_y(value, first):
        return lax.ppermute(value, "gy", swap_pairs(n_y, first))

    def swap_xy(value, first_x, first_y):
        pairs = [
            (sx * n_y + sy, dx * n_y + dy)
            for sx, dx in swap_pairs(n_x, first_x)
            for sy, dy in swap_pairs(n_y, first_y)
        ]
        return lax.ppermute(value, ("mem", "gy"), pairs)

    y_steps = [first for first in (0, 1) if swap_pairs(n_y, first)]

    live = jnp.arange(slots, dtype=jnp.int32) < obs_count[0, 0]
    weight = jnp.where(live, 1.0 / obs_var[0, 0], 0.0)
    col_pos = (obs_slots // rows % cols).astype(f32)
    row_pos = (obs_slots % rows).astype(f32)
    blank = jnp.zeros((META - 4, slots), f32)
    meta = jnp.concatenate([jnp.stack([obs_value[0, 0], weight, col_pos, row_pos]), blank], axis=0)
    meta_row = jnp.stack([meta, swap_x(meta, 0), swap_x(meta, 1)])
    meta_rows = [meta_row] + [swap_y(meta_row, first) for first in y_steps]

    chunks = state.reshape(held, levels, n_x, cols, rows).transpose(2, 0, 1, 3, 4)
    tile = lax.all_to_all(chunks, "mem", split_axis=0, concat_axis=0, tiled=True)
    tile = tile.reshape(members, levels * cols, rows)

    own = gather_call(tile, obs_slots).astype(bf16)
    pair = swap_x(own, 0)
    ens = [own, pair, swap_x(own, 1)]
    both = jnp.stack([own, pair])
    for first in y_steps:
        beside = swap_y(both, first)
        ens += [beside[0], beside[1], swap_xy(own, 1, first)]

    scalars = jnp.stack(
        [lax.axis_index("mem") % 2, lax.axis_index("gy") % 2, radius[0, 0]]
    ).astype(jnp.int32)
    mixing = transform_call(scalars, ens, meta_rows, cols, rows)
    analysed = mix_call(mixing, tile, cols)

    analysed = analysed.reshape(n_x, held, levels, cols, rows)
    back = lax.all_to_all(analysed, "mem", split_axis=0, concat_axis=0, tiled=True)
    return back.transpose(1, 2, 0, 3, 4).reshape(state.shape)


def solution(mesh):
    in_specs = (
        P("mem", None, None, "gy"),
        P("mem", "gy", None),
        P("mem", "gy"),
        P("mem", "gy", None),
        P("mem", "gy", None),
        P("mem", "gy"),
    )
    out_specs = P("mem", None, None, "gy")
    return jax.shard_map(local, mesh=mesh, in_specs=in_specs, out_specs=out_specs, check_vma=False)
```

```python
import functools
import math

import jax
import jax.numpy as jnp
from jax import lax
from jax.experimental import pallas as pl
from jax.experimental.pallas import tpu as pltpu
from jax.sharding import PartitionSpec as P


BLK = 16
NSI = 10
f32 = jnp.float32
bf16 = jnp.bfloat16
META = 8


VMEM = pltpu.MemorySpace.VMEM


def on_chip(*values):
    return [pltpu.with_memory_space_constraint(value, VMEM) for value in values]


def dot(a, b):
    return lax.dot_general(a, b, (((1,), (0,)), ((), ())), preferred_element_type=f32)


def dot_t(a, b):
    return lax.dot_general(a, b, (((1,), (1,)), ((), ())), preferred_element_type=f32)


def split3(x):
    high = x.astype(bf16)
    rest = x - high.astype(f32)
    mid = rest.astype(bf16)
    low = (rest - mid.astype(f32)).astype(bf16)
    return high, mid, low


def gather_kernel(x_ref, idx_ref, ens_ref):
    members, cells, rows = x_ref.shape
    slots = idx_ref.shape[1]
    idx = idx_ref[...]
    row = lax.rem(idx, rows)
    cell = lax.div(idx, rows)
    pick_row = jnp.where(lax.broadcasted_iota(jnp.int32, (rows, slots), 0) == row, 1.0, 0.0).astype(bf16)
    pick_cell = lax.broadcasted_iota(jnp.int32, (cells, slots), 0) == cell
    group = 16
    for first in range(0, members, group):
        found = dot(x_ref[first : first + group].reshape(group * cells, rows), pick_row)
        lines = [
            jnp.sum(jnp.where(pick_cell, found[k * cells : (k + 1) * cells], 0.0), axis=0, keepdims=True)
            for k in range(group)
        ]
        ens_ref[first : first + group, :] = jnp.concatenate(lines, axis=0).astype(bf16)


def gather_call(x, obs_slots):
    vmem = pl.BlockSpec(memory_space=pltpu.VMEM)
    return pl.pallas_call(
        gather_kernel,
        in_specs=[vmem, vmem],
        out_specs=vmem,
        out_shape=pltpu.VMEM((x.shape[0], obs_slots.shape[0]), bf16),
        name="gather",
    )(*on_chip(x), obs_slots[None])


def recursion_product(a, b, left):
    ah, am, al = a
    bh, bm, bl = b
    return dot(
        jnp.concatenate([ah, am, jnp.where(left, al, ah)], axis=1),
        jnp.concatenate([bh, bm, bh, bm, bh, bl], axis=0),
    )


def find_transforms(num_y, sizes, scal_ref, *refs):
    count_r, cols, rows = sizes
    ens_refs = refs[: 2 * num_y]
    meta_refs = refs[2 * num_y : 2 * num_y + 2]
    out_ref, lhs_ref, gram_ref, up_ref, low_ref = refs[2 * num_y + 2 :]
    members, slots = ens_refs[0].shape
    wide = 2 * members
    block_c = scal_ref[0].astype(f32)
    side = scal_ref[1].astype(f32)
    odd_y = scal_ref[2] == 1
    reach = scal_ref[3].astype(f32)
    reach_sq = reach * reach

    def prepare(ens_ref, meta):
        ens = ens_ref[...].astype(f32)
        centre = jnp.sum(ens, axis=0, keepdims=True) * (1.0 / members)
        spread = ens - centre
        sh, sm, sl = split3(spread)
        line = lax.broadcasted_iota(jnp.int32, (members, slots), 0)
        ih, im, il = (part.astype(f32) for part in split3(meta[0:1] - centre))
        extra = jnp.where(line == 0, ih, jnp.where(line == 1, im, jnp.where(line == 2, il, 0.0))).astype(bf16)
        return spread, jnp.concatenate([sh, sm, sl, extra], axis=0)

    def local_weight(meta, dx, dy, block_r):
        gap_c = dx * cols + meta[2:3] - (block_c * float(BLK) + (BLK - 1) / 2.0)
        gap_r = dy * rows + meta[3:4] - (block_r * float(BLK) + (BLK - 1) / 2.0)
        taper = jnp.maximum(1.0 - (gap_c * gap_c + gap_r * gap_r) / reach_sq, 0.0)
        return taper * taper * meta[1:2]

    def put(part, total, column, rho, spread):
        for level, piece in enumerate(split3(rho * spread)):
            start = level * total + part * members
            lhs_ref[start : start + members, column : column + slots] = piece

    def product(y, total, dy, block_r):
        sides = []
        for at, dx in enumerate((0.0, side)):
            meta = meta_refs[at][y]
            spread, rhs = prepare(ens_refs[2 * y + at], meta)
            rho = local_weight(meta, dx, dy, block_r)
            for r in range(total // members):
                put(r, total, at * slots, rho[r : r + 1], spread)
            sides.append(rhs)
        found = dot_t(lhs_ref[: 3 * total, :], jnp.concatenate(sides, axis=1))
        return found[:total] + found[total : 2 * total] + found[2 * total :]

    lines = lax.broadcasted_iota(jnp.int32, (count_r, slots), 0).astype(f32)
    gram_ref[...] = product(0, count_r * members, 0.0, lines).reshape(count_r, members, 4 * members)
    for y in range(1, num_y):
        above = jnp.logical_not(odd_y) if y == 1 else odd_y
        edge = jnp.where(above, count_r - 1, 0)
        gram_ref[edge] += product(y, members, jnp.where(above, 1.0, -1.0), edge.astype(f32))

    line = lax.broadcasted_iota(jnp.int32, (members, wide), 0)
    lane = lax.broadcasted_iota(jnp.int32, (members, wide), 1)
    left = lane < members
    half = jnp.where(lane == line, 1.0, 0.0)
    eye = jnp.where(lane == line + members, 1.0, half)
    blocks = range(count_r)

    def keep(ref, b, value):
        for part, piece in enumerate(split3(value)):
            ref[b, part] = piece

    def held(ref, b):
        return ref[b, 0], ref[b, 1], ref[b, 2]

    scales = []
    drives = []
    starts = []
    for b in blocks:
        found = gram_ref[b]
        high, tail = found[:, :wide], found[:, wide:]
        once = high + jnp.where(left, tail, 0.0)
        system = (members - 1.0) * eye + once + pltpu.roll(once, members, 1)
        drive = jnp.sum(jnp.where(left, 0.0, tail), axis=1, keepdims=True)
        drives.append(jnp.sum(drive * eye, axis=0, keepdims=True))
        scale = jnp.sum(jnp.sum(system * half, axis=1, keepdims=True), axis=0, keepdims=True)
        scales.append(scale)
        starts.append(system / scale)
    for b in blocks:
        factor = 1.5 * eye - 0.5 * starts[b]
        keep(low_ref, b, factor)
        keep(up_ref, b, recursion_product(split3(starts[b]), split3(factor), left))

    def sweep():
        factors = []
        for b in blocks:
            product = recursion_product(held(low_ref, b), held(up_ref, b), left)
            factors.append(split3(1.5 * eye - 0.5 * product))
        for b in blocks:
            upper = recursion_product(held(up_ref, b), factors[b], left)
            lower = recursion_product(factors[b], held(low_ref, b), left)
            keep(up_ref, b, upper)
            keep(low_ref, b, lower)

    together = 3

    def sweeps(_, carry):
        for _ in range(together):
            sweep()
        return carry

    lax.fori_loop(0, (NSI - 1) // together, sweeps, 0)

    mixed = []
    for b in blocks:
        lh, lm, ll = held(low_ref, b)
        lower = lh.astype(f32) + lm.astype(f32) + ll.astype(f32)
        inv_root = lower * lax.rsqrt(scales[b])
        first = jnp.sum(jnp.where(left, inv_root * drives[b], 0.0), axis=1, keepdims=True)
        shift = jnp.sum(inv_root * first, axis=0, keepdims=True)
        transform = math.sqrt(members - 1.0) * inv_root + shift
        mean = jnp.sum(jnp.where(left, transform, 0.0), axis=1, keepdims=True) * (1.0 / members)
        mixed.append(1.0 / members + transform - mean)
    for r in range(0, count_r, 2):
        out_ref[:, r * members : (r + 2) * members] = jnp.where(left, mixed[r], mixed[r + 1]).astype(bf16)


def turn_kernel(x_ref, out_ref):
    for start in range(0, x_ref.shape[1], BLK):
        part = x_ref[:, start : start + BLK, :].astype(f32)
        out_ref[start : start + BLK] = jnp.swapaxes(part, 0, 1).astype(bf16)


def turn_call(x):
    members, cells, rows = x.shape
    vmem = pl.BlockSpec(memory_space=pltpu.VMEM)
    return pl.pallas_call(
        turn_kernel,
        in_specs=[vmem],
        out_specs=vmem,
        out_shape=pltpu.VMEM((cells, members, rows), bf16),
        name="turn",
    )(*on_chip(x))


def mix_cells(levels, cols, scal_ref, mix_ref, x_ref, out_ref):
    _, members, rows = x_ref.shape
    lane_block = lax.broadcasted_iota(jnp.int32, (members, rows), 1) // BLK
    masks = [lane_block == r for r in range(rows // BLK)]
    zero = jnp.zeros((members, rows), bf16)
    mixing = mix_ref[...]
    for level in range(levels):
        start = level * cols + scal_ref[0] * BLK
        found = []
        for c in range(0, BLK, 2):
            wide = []
            for i in range(2):
                x = x_ref[start + c + i]
                wide.append(jnp.concatenate([jnp.where(m, x, zero) for m in masks], axis=0))
            both = dot(mixing, jnp.concatenate(wide, axis=1))
            found += [both[:, :rows], both[:, rows:]]
        out_ref[:, level * BLK : (level + 1) * BLK, :] = jnp.swapaxes(jnp.stack(found), 0, 1).astype(bf16)


def analyse_kernel(num_y, sizes, scal_ref, x_ref, *refs):
    levels, cols, rows = sizes
    column, beside, metas = refs[:num_y], refs[num_y : 2 * num_y], refs[2 * num_y : 2 * num_y + 2]
    out_ref, mix_ref = refs[2 * num_y + 2 : 2 * num_y + 4]
    ens = [ref for both in zip(column, beside) for ref in both]
    find_transforms(num_y, (rows // BLK, float(cols), float(rows)), scal_ref, *ens, *metas, *refs[2 * num_y + 3 :])
    mix_cells(levels, cols, scal_ref, mix_ref, x_ref, out_ref)


def analyse_call(scalars, tile, column, beside, metas, levels, cols):
    num_y = len(column)
    _, members, rows = tile.shape
    slots = column[0].shape[1]
    count_r = rows // BLK
    vmem = pl.BlockSpec(memory_space=pltpu.VMEM)
    return pl.pallas_call(
        functools.partial(analyse_kernel, num_y, (levels, cols, rows)),
        in_specs=[pl.BlockSpec(memory_space=pltpu.SMEM)] + [vmem] * (2 * num_y + 3),
        out_specs=vmem,
        out_shape=pltpu.VMEM((members, levels * BLK, rows), bf16),
        scratch_shapes=[
            pltpu.VMEM((members, count_r * members), bf16),
            pltpu.VMEM((3 * count_r * members, 2 * slots), bf16),
            pltpu.VMEM((count_r, members, 4 * members), f32),
            pltpu.VMEM((count_r, 3, members, 2 * members), bf16),
            pltpu.VMEM((count_r, 3, members, 2 * members), bf16),
        ],
        cost_estimate=pl.CostEstimate(flops=4 * 10**9, transcendentals=0, bytes_accessed=2 * 10**6),
        name="analyse",
    )(scalars, *on_chip(tile, *column, *beside, *metas))


def pack_kernel(state_ref, out_ref, sems):
    count, _, _, cols, _ = out_ref.shape
    copies = [
        pltpu.make_async_copy(state_ref.at[:, :, pl.ds(p * cols, cols), :], out_ref.at[p], sems.at[p]) for p in range(count)
    ]
    for copy in copies:
        copy.start()
    for copy in copies:
        copy.wait()


def pack_call(state, count, cols):
    held, levels, _, rows = state.shape
    return pl.pallas_call(
        pack_kernel,
        in_specs=[pl.BlockSpec(memory_space=pl.ANY)],
        out_specs=pl.BlockSpec(memory_space=pltpu.VMEM),
        out_shape=pltpu.VMEM((count, held, levels, cols, rows), bf16),
        scratch_shapes=[pltpu.SemaphoreType.DMA((count,))],
        name="pack",
    )(state)


def unpack_kernel(first_ref, second_ref, out_ref, sems):
    count, _, _, half, _ = first_ref.shape
    copies = []
    for p in range(count):
        for at, ref in enumerate((second_ref, first_ref) if p % 2 == 0 else (first_ref, second_ref)):
            start = (2 * p + at) * half
            copies.append(pltpu.make_async_copy(ref.at[p], out_ref.at[:, :, pl.ds(start, half), :], sems.at[2 * p + at]))
    for copy in copies:
        copy.start()
    for copy in copies:
        copy.wait()


def unpack_call(first, second):
    count, held, levels, half, rows = first.shape
    vmem = pl.BlockSpec(memory_space=pltpu.VMEM)
    return pl.pallas_call(
        unpack_kernel,
        in_specs=[vmem, vmem],
        out_specs=pl.BlockSpec(memory_space=pl.ANY),
        out_shape=jax.ShapeDtypeStruct((held, levels, 2 * count * half, rows), bf16),
        scratch_shapes=[pltpu.SemaphoreType.DMA((2 * count,))],
        name="unpack",
    )(*on_chip(first, second))


def swap_pairs(count, first):
    pairs = []
    for i in range(first, count - 1, 2):
        pairs += [(i, i + 1), (i + 1, i)]
    return pairs


def local(state, obs_index, obs_count, obs_value, obs_var, radius):
    n_x = lax.axis_size("mem")
    n_y = lax.axis_size("gy")
    held, levels, all_cols, rows = state.shape
    cols = all_cols // n_x
    members = held * n_x
    assert cols == 2 * BLK
    obs_slots = obs_index[0, 0]
    slots = obs_slots.shape[0]

    def swap_x(value, first):
        return lax.ppermute(value, "mem", swap_pairs(n_x, first))

    def swap_y(value, first):
        return lax.ppermute(value, "gy", swap_pairs(n_y, first))

    y_steps = [first for first in (0, 1) if swap_pairs(n_y, first)]

    live = jnp.arange(slots, dtype=jnp.int32) < obs_count[0, 0]
    weight = jnp.where(live, 1.0 / obs_var[0, 0], 0.0)
    col_pos = (obs_slots // rows % cols).astype(f32)
    row_pos = (obs_slots % rows).astype(f32)
    blank = jnp.zeros((META - 4, slots), f32)
    meta = jnp.concatenate([jnp.stack([obs_value[0, 0], weight, col_pos, row_pos]), blank], axis=0)
    meta_column = jnp.stack([meta] + [swap_y(meta, first) for first in y_steps])
    near_meta = swap_x(meta_column, 0)
    far_meta = swap_x(meta_column, 1)
    odd_x = lax.axis_index("mem") & 1
    odd_y = lax.axis_index("gy") & 1
    scalars = [
        jnp.stack([block_c, 2 * block_c - 1, odd_y, radius[0, 0]]).astype(jnp.int32) for block_c in (1 - odd_x, odd_x)
    ]

    tile = lax.all_to_all(pack_call(state, n_x, cols), "mem", split_axis=0, concat_axis=0, tiled=True)
    tile, meta_column, near_meta, scalars = lax.optimization_barrier((tile, meta_column, near_meta, scalars))
    tile = tile.reshape(members, levels * cols, rows)

    own = gather_call(tile, obs_slots)
    column = [own] + [swap_y(own, first) for first in y_steps]
    far_own = swap_x(own, 1)
    tile = turn_call(tile)
    near = [swap_x(ens, 0) for ens in column]

    def send_back(analysed):
        analysed = analysed.reshape(n_x, held, levels, BLK, rows)
        return lax.all_to_all(analysed, "mem", split_axis=0, concat_axis=0, tiled=True)

    analysed = analyse_call(scalars[0], tile, column, near, (meta_column, near_meta), levels, cols)
    first = send_back(analysed)
    far = [far_own] + [swap_y(far_own, step) for step in y_steps]
    analysed = analyse_call(scalars[1], tile, column, far, (meta_column, far_meta), levels, cols)
    second = send_back(analysed)
    return unpack_call(first, second)


def solution(mesh):
    in_specs = (
        P("mem", None, None, "gy"),
        P("mem", "gy", None),
        P("mem", "gy"),
        P("mem", "gy", None),
        P("mem", "gy", None),
        P("mem", "gy"),
    )
    out_specs = P("mem", None, None, "gy")
    return jax.shard_map(local, mesh=mesh, in_specs=in_specs, out_specs=out_specs, check_vma=False)
```

```python
import functools
import math

import jax
import jax.numpy as jnp
from jax import lax
from jax.experimental import pallas as pl
from jax.experimental.pallas import tpu as pltpu
from jax.sharding import PartitionSpec as P


BLK = 16
NSI = 10
f32 = jnp.float32
bf16 = jnp.bfloat16
META = 8


VMEM = pltpu.MemorySpace.VMEM


def on_chip(*values):
    return [pltpu.with_memory_space_constraint(value, VMEM) for value in values]


def dot(a, b):
    return lax.dot_general(a, b, (((1,), (0,)), ((), ())), preferred_element_type=f32)


def dot_t(a, b):
    return lax.dot_general(a, b, (((1,), (1,)), ((), ())), preferred_element_type=f32)


def split3(x):
    high = x.astype(bf16)
    rest = x - high.astype(f32)
    mid = rest.astype(bf16)
    low = (rest - mid.astype(f32)).astype(bf16)
    return high, mid, low


def gather_kernel(x_ref, idx_ref, ens_ref):
    members, cells, rows = x_ref.shape
    slots = idx_ref.shape[1]
    idx = idx_ref[...]
    row = lax.rem(idx, rows)
    cell = lax.div(idx, rows)
    pick_row = jnp.where(lax.broadcasted_iota(jnp.int32, (rows, slots), 0) == row, 1.0, 0.0).astype(bf16)
    pick_cell = lax.broadcasted_iota(jnp.int32, (cells, slots), 0) == cell
    group = 16
    for first in range(0, members, group):
        found = dot(x_ref[first : first + group].reshape(group * cells, rows), pick_row)
        lines = [
            jnp.sum(jnp.where(pick_cell, found[k * cells : (k + 1) * cells], 0.0), axis=0, keepdims=True)
            for k in range(group)
        ]
        ens_ref[first : first + group, :] = jnp.concatenate(lines, axis=0).astype(bf16)


def gather_call(x, obs_slots):
    vmem = pl.BlockSpec(memory_space=pltpu.VMEM)
    return pl.pallas_call(
        gather_kernel,
        in_specs=[vmem, vmem],
        out_specs=vmem,
        out_shape=pltpu.VMEM((x.shape[0], obs_slots.shape[0]), bf16),
        name="gather",
    )(*on_chip(x), obs_slots[None])


def recursion_product(a, b, left):
    ah, am, al = a
    bh, bm, bl = b
    return dot(
        jnp.concatenate([ah, am, jnp.where(left, al, ah)], axis=1),
        jnp.concatenate([bh, bm, bh, bm, bh, bl], axis=0),
    )


def short_product(a, b):
    return dot(jnp.concatenate([a[0], a[1]], axis=1), jnp.concatenate([b[0], b[1], b[0], b[1]], axis=0))


def find_transforms(num_y, sizes, scal_ref, *refs):
    count_r, cols, rows = sizes
    ens_refs = refs[: 2 * num_y]
    meta_refs = refs[2 * num_y : 2 * num_y + 2]
    out_ref, lhs_ref, gram_ref, up_ref, low_ref = refs[2 * num_y + 2 :]
    members, slots = ens_refs[0].shape
    wide = 2 * members
    block_c = scal_ref[0].astype(f32)
    side = scal_ref[1].astype(f32)
    odd_y = scal_ref[2] == 1
    reach = scal_ref[3].astype(f32)
    reach_sq = reach * reach

    def prepare(ens_ref, meta):
        ens = ens_ref[...].astype(f32)
        centre = jnp.sum(ens, axis=0, keepdims=True) * (1.0 / members)
        spread = ens - centre
        parts = [*split3(spread), jnp.zeros((members, slots), bf16)]
        return spread, meta[0:1] - centre, jnp.concatenate(parts, axis=0)

    def local_weight(meta, dx, dy, block_r):
        gap_c = dx * cols + meta[2:3] - (block_c * float(BLK) + (BLK - 1) / 2.0)
        gap_r = dy * rows + meta[3:4] - (block_r * float(BLK) + (BLK - 1) / 2.0)
        taper = jnp.maximum(1.0 - (gap_c * gap_c + gap_r * gap_r) / reach_sq, 0.0)
        return taper * taper * meta[1:2]

    def put(part, total, column, rho, spread):
        for level, piece in enumerate(split3(rho * spread)):
            start = level * total + part * members
            lhs_ref[start : start + members, column : column + slots] = piece

    lines = lax.broadcasted_iota(jnp.int32, (count_r, slots), 0)

    def product(y, total, dy, block_r, chosen):
        sides = []
        forces = []
        for at, dx in enumerate((0.0, side)):
            meta = meta_refs[at][y]
            spread, innovation, rhs = prepare(ens_refs[2 * y + at], meta)
            rho = local_weight(meta, dx, dy, block_r)
            for r in range(total // members):
                put(r, total, at * slots, rho[r : r + 1], spread)
            force = rho * innovation
            forces.append(force if chosen is None else jnp.where(chosen, force, 0.0))
            sides.append(rhs)
        rhs = jnp.concatenate(sides, axis=1)
        force = [part.astype(f32) for part in split3(jnp.concatenate(forces, axis=1))]
        drive = dot_t(jnp.concatenate(force, axis=0).astype(bf16), rhs)
        drive = drive[:count_r] + drive[count_r : 2 * count_r] + drive[2 * count_r :]
        found = dot_t(lhs_ref[: 3 * total, :], rhs)
        return found[:total] + found[total : 2 * total] + found[2 * total :], drive

    found, drive = product(0, count_r * members, 0.0, lines.astype(f32), None)
    gram_ref[...] = found.reshape(count_r, members, 4 * members)
    for y in range(1, num_y):
        above = jnp.logical_not(odd_y) if y == 1 else odd_y
        edge = jnp.where(above, count_r - 1, 0)
        found, more = product(y, members, jnp.where(above, 1.0, -1.0), edge.astype(f32), lines == edge)
        gram_ref[edge] += found
        drive += more
    drive = drive[:, :wide] + drive[:, wide:]
    drive = drive + pltpu.roll(drive, members, 1)

    line = lax.broadcasted_iota(jnp.int32, (members, wide), 0)
    lane = lax.broadcasted_iota(jnp.int32, (members, wide), 1)
    left = lane < members
    half = jnp.where(lane == line, 1.0, 0.0)
    eye = jnp.where(lane == line + members, 1.0, half)
    blocks = range(count_r)

    def keep(ref, b, value):
        for part, piece in enumerate(split3(value)):
            ref[b, part] = piece

    def held(ref, b):
        return ref[b, 0], ref[b, 1], ref[b, 2]

    scales = []
    drives = []
    starts = []
    for b in blocks:
        found = gram_ref[b]
        once = found[:, :wide] + found[:, wide:]
        system = (members - 1.0) * eye + once + pltpu.roll(once, members, 1)
        drives.append(drive[b : b + 1])
        scale = jnp.sum(jnp.sum(system * half, axis=0, keepdims=True), axis=1, keepdims=True)
        scales.append(scale)
        starts.append(system / scale)
    for b in blocks:
        factor = 1.5 * eye - 0.5 * starts[b]
        keep(low_ref, b, factor)
        keep(up_ref, b, recursion_product(split3(starts[b]), split3(factor), left))

    def first_stage(b):
        return split3(1.5 * eye - 0.5 * short_product(held(low_ref, b), held(up_ref, b)))

    def second_stage(b, factor, last):
        lower = recursion_product(factor, held(low_ref, b), left)
        if not last:
            upper = recursion_product(held(up_ref, b), factor, left)
            keep(up_ref, b, upper)
            keep(low_ref, b, lower)
        return lower

    lag = count_r // 2
    steps = (NSI - 1) * count_r
    factors = {}
    lowers = []
    for step in range(steps + lag):
        if step < steps:
            factors[step] = first_stage(step % count_r)
        done = step - lag
        if done >= 0:
            last = done >= steps - count_r
            lower = second_stage(done % count_r, factors.pop(done), last)
            if last:
                lowers.append(lower)

    mixed = []
    for b in blocks:
        inv_root = lowers[b] * lax.rsqrt(scales[b])
        first = jnp.sum(jnp.where(left, inv_root * drives[b], 0.0), axis=1, keepdims=True)
        shift = jnp.sum(inv_root * first, axis=0, keepdims=True)
        transform = math.sqrt(members - 1.0) * inv_root + shift
        mean = jnp.sum(jnp.where(left, transform, 0.0), axis=1, keepdims=True) * (1.0 / members)
        mixed.append(1.0 / members + transform - mean)
    for r in range(0, count_r, 2):
        out_ref[:, r * members : (r + 2) * members] = jnp.where(left, mixed[r], mixed[r + 1]).astype(bf16)


def turn_kernel(x_ref, out_ref):
    for start in range(0, x_ref.shape[1], BLK):
        part = x_ref[:, start : start + BLK, :].astype(f32)
        out_ref[start : start + BLK] = jnp.swapaxes(part, 0, 1).astype(bf16)


def turn_call(x):
    members, cells, rows = x.shape
    vmem = pl.BlockSpec(memory_space=pltpu.VMEM)
    return pl.pallas_call(
        turn_kernel,
        in_specs=[vmem],
        out_specs=vmem,
        out_shape=pltpu.VMEM((cells, members, rows), bf16),
        name="turn",
    )(*on_chip(x))


def mix_cells(levels, cols, scal_ref, mix_ref, x_ref, out_ref):
    _, members, rows = x_ref.shape
    lane_block = lax.broadcasted_iota(jnp.int32, (members, rows), 1) // BLK
    masks = [jnp.where(lane_block == r, 1.0, 0.0).astype(bf16) for r in range(rows // BLK)]
    mixing = mix_ref[...]
    for level in range(levels):
        start = level * cols + scal_ref[0] * BLK
        found = []
        for c in range(0, BLK, 2):
            wide = []
            for i in range(2):
                x = x_ref[start + c + i]
                wide.append(jnp.concatenate([x * mask for mask in masks], axis=0))
            both = dot(mixing, jnp.concatenate(wide, axis=1))
            found += [both[:, :rows], both[:, rows:]]
        out_ref[:, level * BLK : (level + 1) * BLK, :] = jnp.swapaxes(jnp.stack(found), 0, 1).astype(bf16)


def analyse_kernel(num_y, sizes, scal_ref, x_ref, *refs):
    levels, cols, rows = sizes
    column, beside, metas = refs[:num_y], refs[num_y : 2 * num_y], refs[2 * num_y : 2 * num_y + 2]
    out_ref, mix_ref = refs[2 * num_y + 2 : 2 * num_y + 4]
    ens = [ref for both in zip(column, beside) for ref in both]
    find_transforms(num_y, (rows // BLK, float(cols), float(rows)), scal_ref, *ens, *metas, *refs[2 * num_y + 3 :])
    mix_cells(levels, cols, scal_ref, mix_ref, x_ref, out_ref)


def analyse_call(scalars, tile, column, beside, metas, levels, cols):
    num_y = len(column)
    _, members, rows = tile.shape
    slots = column[0].shape[1]
    count_r = rows // BLK
    vmem = pl.BlockSpec(memory_space=pltpu.VMEM)
    return pl.pallas_call(
        functools.partial(analyse_kernel, num_y, (levels, cols, rows)),
        in_specs=[pl.BlockSpec(memory_space=pltpu.SMEM)] + [vmem] * (2 * num_y + 3),
        out_specs=vmem,
        out_shape=pltpu.VMEM((members, levels * BLK, rows), bf16),
        scratch_shapes=[
            pltpu.VMEM((members, count_r * members), bf16),
            pltpu.VMEM((3 * count_r * members, 2 * slots), bf16),
            pltpu.VMEM((count_r, members, 4 * members), f32),
            pltpu.VMEM((count_r, 3, members, 2 * members), bf16),
            pltpu.VMEM((count_r, 3, members, 2 * members), bf16),
        ],
        cost_estimate=pl.CostEstimate(flops=4 * 10**9, transcendentals=0, bytes_accessed=2 * 10**6),
        name="analyse",
    )(scalars, *on_chip(tile, *column, *beside, *metas))


def pack_kernel(state_ref, out_ref, held_ref, in_sems, out_sems):
    count, _, _, cols, _ = out_ref.shape
    loads = [
        pltpu.make_async_copy(state_ref.at[:, :, pl.ds(p * cols, cols), :], held_ref.at[p], in_sems.at[p])
        for p in range(count)
    ]
    stores = [pltpu.make_async_copy(held_ref.at[p], out_ref.at[p], out_sems.at[p]) for p in range(count)]
    for load in loads:
        load.start()
    for load, store in zip(loads, stores):
        load.wait()
        store.start()
    for store in stores:
        store.wait()


def pack_call(state, count, cols):
    held, levels, _, rows = state.shape
    shape = (count, held, levels, cols, rows)
    return pl.pallas_call(
        pack_kernel,
        in_specs=[pl.BlockSpec(memory_space=pl.ANY)],
        out_specs=pl.BlockSpec(memory_space=pl.ANY),
        out_shape=jax.ShapeDtypeStruct(shape, bf16),
        scratch_shapes=[pltpu.VMEM(shape, bf16), pltpu.SemaphoreType.DMA((count,)), pltpu.SemaphoreType.DMA((count,))],
        name="pack",
    )(state)


def unpack_kernel(near, half_ref, *refs):
    out_ref, sems = refs[-2:]
    count, _, _, half, _ = half_ref.shape
    copies = []
    for p in range(count):
        start = (2 * p + (p + near) % 2) * half
        copies.append(pltpu.make_async_copy(half_ref.at[p], out_ref.at[:, :, pl.ds(start, half), :], sems.at[p]))
    for copy in copies:
        copy.start()
    for copy in copies:
        copy.wait()


def unpack_call(near, part, whole=None):
    count, held, levels, half, rows = part.shape
    anywhere = pl.BlockSpec(memory_space=pl.ANY)
    others = [] if whole is None else [whole]
    return pl.pallas_call(
        functools.partial(unpack_kernel, near),
        in_specs=[pl.BlockSpec(memory_space=pltpu.VMEM)] + [anywhere] * len(others),
        out_specs=anywhere,
        out_shape=jax.ShapeDtypeStruct((held, levels, 2 * count * half, rows), bf16),
        scratch_shapes=[pltpu.SemaphoreType.DMA((count,))],
        input_output_aliases={1: 0} if others else {},
        name="unpack",
    )(*on_chip(part), *others)


def swap_pairs(count, first):
    pairs = []
    for i in range(first, count - 1, 2):
        pairs += [(i, i + 1), (i + 1, i)]
    return pairs


def local(state, obs_index, obs_count, obs_value, obs_var, radius):
    n_x = lax.axis_size("mem")
    n_y = lax.axis_size("gy")
    held, levels, all_cols, rows = state.shape
    cols = all_cols // n_x
    members = held * n_x
    assert cols == 2 * BLK
    obs_slots = obs_index[0, 0]
    slots = obs_slots.shape[0]

    def swap_x(value, first):
        return lax.ppermute(value, "mem", swap_pairs(n_x, first))

    def swap_y(value, first):
        return lax.ppermute(value, "gy", swap_pairs(n_y, first))

    y_steps = [first for first in (0, 1) if swap_pairs(n_y, first)]

    live = jnp.arange(slots, dtype=jnp.int32) < obs_count[0, 0]
    weight = jnp.where(live, 1.0 / obs_var[0, 0], 0.0)
    col_pos = (obs_slots // rows % cols).astype(f32)
    row_pos = (obs_slots % rows).astype(f32)
    blank = jnp.zeros((META - 4, slots), f32)
    meta = jnp.concatenate([jnp.stack([obs_value[0, 0], weight, col_pos, row_pos]), blank], axis=0)
    meta_column = jnp.stack([meta] + [swap_y(meta, first) for first in y_steps])
    near_meta = swap_x(meta_column, 0)
    far_meta = swap_x(meta_column, 1)
    odd_x = lax.axis_index("mem") & 1
    odd_y = lax.axis_index("gy") & 1
    scalars = [
        jnp.stack([block_c, 2 * block_c - 1, odd_y, radius[0, 0]]).astype(jnp.int32) for block_c in (1 - odd_x, odd_x)
    ]

    tile = lax.all_to_all(pack_call(state, n_x, cols), "mem", split_axis=0, concat_axis=0, tiled=True)
    tile, meta_column, near_meta, scalars = lax.optimization_barrier((tile, meta_column, near_meta, scalars))
    tile = tile.reshape(members, levels * cols, rows)

    own = gather_call(tile, obs_slots)
    column = [own] + [swap_y(own, first) for first in y_steps]
    far_own = swap_x(own, 1)
    tile = turn_call(tile)
    near = [swap_x(ens, 0) for ens in column]

    def send_back(analysed):
        analysed = analysed.reshape(n_x, held, levels, BLK, rows)
        return lax.all_to_all(analysed, "mem", split_axis=0, concat_axis=0, tiled=True)

    analysed = analyse_call(scalars[0], tile, column, near, (meta_column, near_meta), levels, cols)
    first = send_back(analysed)
    far = [far_own] + [swap_y(far_own, step) for step in y_steps]
    analysed = analyse_call(scalars[1], tile, column, far, (meta_column, far_meta), levels, cols)
    second = send_back(analysed)
    whole = unpack_call(1, first)
    return unpack_call(0, second, whole)


def solution(mesh):
    in_specs = (
        P("mem", None, None, "gy"),
        P("mem", "gy", None),
        P("mem", "gy"),
        P("mem", "gy", None),
        P("mem", "gy", None),
        P("mem", "gy"),
    )
    out_specs = P("mem", None, None, "gy")
    return jax.shard_map(local, mesh=mesh, in_specs=in_specs, out_specs=out_specs, check_vma=False)
```

```python
import functools
import math

import jax
import jax.numpy as jnp
from jax import lax
from jax.experimental import pallas as pl
from jax.experimental.pallas import tpu as pltpu
from jax.sharding import PartitionSpec as P


BLK = 16
NSI = 10
f32 = jnp.float32
bf16 = jnp.bfloat16
PITCH = BLK + 8
META = 8


VMEM = pltpu.MemorySpace.VMEM


def on_chip(*values):
    return [pltpu.with_memory_space_constraint(value, VMEM) for value in values]


def dot(a, b):
    return lax.dot_general(a, b, (((1,), (0,)), ((), ())), preferred_element_type=f32)


def dot_t(a, b):
    return lax.dot_general(a, b, (((1,), (1,)), ((), ())), preferred_element_type=f32)


def split3(x):
    high = x.astype(bf16)
    rest = x - high.astype(f32)
    mid = rest.astype(bf16)
    low = (rest - mid.astype(f32)).astype(bf16)
    return high, mid, low


def gather_kernel(x_ref, idx_ref, ens_ref):
    members, cells, rows = x_ref.shape
    slots = idx_ref.shape[1]
    idx = idx_ref[...]
    row = lax.rem(idx, rows)
    cell = lax.div(idx, rows)
    pick_row = jnp.where(lax.broadcasted_iota(jnp.int32, (rows, slots), 0) == row, 1.0, 0.0).astype(bf16)
    pick_cell = lax.broadcasted_iota(jnp.int32, (cells, slots), 0) == cell
    group = 16
    for first in range(0, members, group):
        found = dot(x_ref[first : first + group].reshape(group * cells, rows), pick_row)
        lines = [
            jnp.sum(jnp.where(pick_cell, found[k * cells : (k + 1) * cells], 0.0), axis=0, keepdims=True)
            for k in range(group)
        ]
        ens_ref[first : first + group, :] = jnp.concatenate(lines, axis=0).astype(bf16)


def gather_call(x, obs_slots):
    vmem = pl.BlockSpec(memory_space=pltpu.VMEM)
    return pl.pallas_call(
        gather_kernel,
        in_specs=[vmem, vmem],
        out_specs=vmem,
        out_shape=pltpu.VMEM((x.shape[0], obs_slots.shape[0]), bf16),
        name="gather",
    )(*on_chip(x, obs_slots[None]))


def recursion_product(a, b, left):
    ah, am, al = a
    bh, bm, bl = b
    return dot(
        jnp.concatenate([ah, am, jnp.where(left, al, ah)], axis=1),
        jnp.concatenate([bh, bm, bh, bm, bh, bl], axis=0),
    )


def short_product(a, b):
    return dot(jnp.concatenate([a[0], a[1]], axis=1), jnp.concatenate([b[0], b[1], b[0], b[1]], axis=0))


def find_transforms(num_y, sizes, block_c, *refs):
    count_r, cols, rows = sizes
    ens_refs = refs[: 2 * num_y]
    meta_refs = refs[2 * num_y : 2 * num_y + 2]
    out_ref, lhs_ref, gram_ref, up_ref, low_ref = refs[2 * num_y + 2 :]
    members, slots = ens_refs[0].shape
    wide = 2 * members
    side = (2 * block_c - 1).astype(f32)
    block_c = block_c.astype(f32)
    odd_y = lax.rem(lax.axis_index("gy"), 2) == 1
    reach = meta_refs[0][0, 4:5]
    reach_sq = reach * reach

    def prepare(ens_ref, meta):
        ens = ens_ref[...].astype(f32)
        centre = jnp.sum(ens, axis=0, keepdims=True) * (1.0 / members)
        spread = ens - centre
        parts = [*split3(spread), jnp.zeros((members, slots), bf16)]
        return spread, meta[0:1] - centre, jnp.concatenate(parts, axis=0)

    def local_weight(meta, dx, dy, block_r):
        gap_c = dx * cols + meta[2:3] - (block_c * float(BLK) + (BLK - 1) / 2.0)
        gap_r = dy * rows + meta[3:4] - (block_r * float(BLK) + (BLK - 1) / 2.0)
        taper = jnp.maximum(1.0 - (gap_c * gap_c + gap_r * gap_r) / reach_sq, 0.0)
        return taper * taper * meta[1:2]

    def put(part, total, column, rho, spread):
        for level, piece in enumerate(split3(rho * spread)):
            start = level * total + part * members
            lhs_ref[start : start + members, column : column + slots] = piece

    lines = lax.broadcasted_iota(jnp.int32, (count_r, slots), 0)

    def product(y, total, dy, block_r, chosen):
        sides = []
        forces = []
        for at, dx in enumerate((0.0, side)):
            meta = meta_refs[at][y]
            spread, innovation, rhs = prepare(ens_refs[2 * y + at], meta)
            rho = local_weight(meta, dx, dy, block_r)
            for r in range(total // members):
                put(r, total, at * slots, rho[r : r + 1], spread)
            force = rho * innovation
            forces.append(force if chosen is None else jnp.where(chosen, force, 0.0))
            sides.append(rhs)
        rhs = jnp.concatenate(sides, axis=1)
        force = [part.astype(f32) for part in split3(jnp.concatenate(forces, axis=1))]
        drive = dot_t(jnp.concatenate(force, axis=0).astype(bf16), rhs)
        drive = drive[:count_r] + drive[count_r : 2 * count_r] + drive[2 * count_r :]
        found = dot_t(lhs_ref[: 3 * total, :], rhs)
        return found[:total] + found[total : 2 * total] + found[2 * total :], drive

    found, drive = product(0, count_r * members, 0.0, lines.astype(f32), None)
    gram_ref[...] = found.reshape(count_r, members, 4 * members)
    for y in range(1, num_y):
        above = jnp.logical_not(odd_y) if y == 1 else odd_y
        edge = jnp.where(above, count_r - 1, 0)
        found, more = product(y, members, jnp.where(above, 1.0, -1.0), edge.astype(f32), lines == edge)
        gram_ref[edge] += found
        drive += more
    drive = drive[:, :wide] + drive[:, wide:]
    drive = drive + pltpu.roll(drive, members, 1)

    line = lax.broadcasted_iota(jnp.int32, (members, wide), 0)
    lane = lax.broadcasted_iota(jnp.int32, (members, wide), 1)
    left = lane < members
    half = jnp.where(lane == line, 1.0, 0.0)
    eye = jnp.where(lane == line + members, 1.0, half)
    blocks = range(count_r)

    def keep(ref, b, value):
        for part, piece in enumerate(split3(value)):
            ref[b, part] = piece

    def held(ref, b):
        return ref[b, 0], ref[b, 1], ref[b, 2]

    scales = []
    drives = []
    starts = []
    for b in blocks:
        found = gram_ref[b]
        once = found[:, :wide] + found[:, wide:]
        system = (members - 1.0) * eye + once + pltpu.roll(once, members, 1)
        drives.append(drive[b : b + 1])
        scale = jnp.sum(jnp.sum(system * half, axis=0, keepdims=True), axis=1, keepdims=True)
        scales.append(scale)
        starts.append(system / scale)
    for b in blocks:
        factor = 1.5 * eye - 0.5 * starts[b]
        keep(low_ref, b, factor)
        keep(up_ref, b, recursion_product(split3(starts[b]), split3(factor), left))

    def first_stage(b):
        return split3(1.5 * eye - 0.5 * short_product(held(low_ref, b), held(up_ref, b)))

    def second_stage(b, factor, last):
        lower = recursion_product(factor, held(low_ref, b), left)
        if not last:
            upper = recursion_product(held(up_ref, b), factor, left)
            keep(up_ref, b, upper)
            keep(low_ref, b, lower)
        return lower

    lag = count_r // 2
    steps = (NSI - 1) * count_r
    factors = {}
    lowers = []
    for step in range(steps + lag):
        if step < steps:
            factors[step] = first_stage(step % count_r)
        done = step - lag
        if done >= 0:
            last = done >= steps - count_r
            lower = second_stage(done % count_r, factors.pop(done), last)
            if last:
                lowers.append(lower)

    mixed = []
    for b in blocks:
        inv_root = lowers[b] * lax.rsqrt(scales[b])
        first = jnp.sum(jnp.where(left, inv_root * drives[b], 0.0), axis=1, keepdims=True)
        shift = jnp.sum(inv_root * first, axis=0, keepdims=True)
        transform = math.sqrt(members - 1.0) * inv_root + shift
        mean = jnp.sum(jnp.where(left, transform, 0.0), axis=1, keepdims=True) * (1.0 / members)
        mixed.append(1.0 / members + transform - mean)
    for r in range(0, count_r, 2):
        out_ref[:, r * members : (r + 2) * members] = jnp.where(left, mixed[r], mixed[r + 1]).astype(bf16)


def turn_kernel(x_ref, out_ref):
    for start in range(0, x_ref.shape[1], BLK):
        part = x_ref[:, start : start + BLK, :].astype(f32)
        out_ref[start : start + BLK] = jnp.swapaxes(part, 0, 1).astype(bf16)


def turn_call(x):
    members, cells, rows = x.shape
    vmem = pl.BlockSpec(memory_space=pltpu.VMEM)
    return pl.pallas_call(
        turn_kernel,
        in_specs=[vmem],
        out_specs=vmem,
        out_shape=pltpu.VMEM((cells, members, rows), bf16),
        name="turn",
    )(*on_chip(x))


def mix_cells(levels, cols, block_c, mix_ref, x_ref, out_ref, held_ref, ready_ref, sems):
    _, members, rows = x_ref.shape
    lane_block = lax.broadcasted_iota(jnp.int32, (members, rows), 1) // BLK
    masks = [jnp.where(lane_block == r, 1.0, 0.0).astype(bf16) for r in range(rows // BLK)]
    mixing = mix_ref[...]
    copies = []
    for level in range(levels):
        start = level * cols + block_c * BLK
        for c in range(0, BLK, 2):
            wide = []
            for i in range(2):
                x = x_ref[start + c + i]
                wide.append(jnp.concatenate([x * mask for mask in masks], axis=0))
            both = dot(mixing, jnp.concatenate(wide, axis=1))
            for i in range(2):
                held_ref[level, pl.ds(c + i, members, stride=PITCH), :] = both[:, i * rows : (i + 1) * rows]
        mixed = held_ref[level].reshape(members, PITCH, rows)[:, :BLK, :]
        ready_ref[level] = mixed.astype(bf16)
        part = out_ref.at[:, pl.ds(level * BLK, BLK), :]
        copies.append(pltpu.make_async_copy(ready_ref.at[level], part, sems.at[level]))
        copies[-1].start()
    for copy in copies:
        copy.wait()


def analyse_kernel(num_y, far, sizes, x_ref, *refs):
    levels, cols, rows = sizes
    block_c = lax.rem(lax.axis_index("mem") + (0 if far else 1), 2)
    column, beside, metas = refs[:num_y], refs[num_y : 2 * num_y], refs[2 * num_y : 2 * num_y + 2]
    out_ref, mix_ref = refs[2 * num_y + 2 : 2 * num_y + 4]
    ens = [ref for both in zip(column, beside) for ref in both]
    find_transforms(num_y, (rows // BLK, float(cols), float(rows)), block_c, *ens, *metas, *refs[2 * num_y + 3 : -3])
    mix_cells(levels, cols, block_c, mix_ref, x_ref, out_ref, *refs[-3:])


def analyse_call(far, tile, column, beside, metas, levels, cols):
    num_y = len(column)
    _, members, rows = tile.shape
    slots = column[0].shape[1]
    count_r = rows // BLK
    vmem = pl.BlockSpec(memory_space=pltpu.VMEM)
    return pl.pallas_call(
        functools.partial(analyse_kernel, num_y, far, (levels, cols, rows)),
        in_specs=[vmem] * (2 * num_y + 3),
        out_specs=pl.BlockSpec(memory_space=pl.ANY),
        out_shape=jax.ShapeDtypeStruct((members, levels * BLK, rows), bf16),
        scratch_shapes=[
            pltpu.VMEM((members, count_r * members), bf16),
            pltpu.VMEM((3 * count_r * members, 2 * slots), bf16),
            pltpu.VMEM((count_r, members, 4 * members), f32),
            pltpu.VMEM((count_r, 3, members, 2 * members), bf16),
            pltpu.VMEM((count_r, 3, members, 2 * members), bf16),
            pltpu.VMEM((levels, members * PITCH, rows), f32),
            pltpu.VMEM((levels, members, BLK, rows), bf16),
            pltpu.SemaphoreType.DMA((levels,)),
        ],
        cost_estimate=pl.CostEstimate(flops=4 * 10**9, transcendentals=0, bytes_accessed=2 * 10**6),
        name="analyse",
    )(*on_chip(tile, *column, *beside, *metas))


def pack_kernel(state_ref, out_ref, held_ref, in_sems, out_sems):
    count, _, _, cols, _ = out_ref.shape
    loads = [
        pltpu.make_async_copy(state_ref.at[:, :, pl.ds(p * cols, cols), :], held_ref.at[p], in_sems.at[p])
        for p in range(count)
    ]
    stores = [pltpu.make_async_copy(held_ref.at[p], out_ref.at[p], out_sems.at[p]) for p in range(count)]
    for load in loads:
        load.start()
    for load, store in zip(loads, stores):
        load.wait()
        store.start()
    for store in stores:
        store.wait()


def pack_call(state, count, cols):
    held, levels, _, rows = state.shape
    shape = (count, held, levels, cols, rows)
    return pl.pallas_call(
        pack_kernel,
        in_specs=[pl.BlockSpec(memory_space=pl.ANY)],
        out_specs=pl.BlockSpec(memory_space=pl.ANY),
        out_shape=jax.ShapeDtypeStruct(shape, bf16),
        scratch_shapes=[pltpu.VMEM(shape, bf16), pltpu.SemaphoreType.DMA((count,)), pltpu.SemaphoreType.DMA((count,))],
        name="pack",
    )(state)


def unpack_kernel(near, half_ref, *refs):
    out_ref, sems = refs[-2:]
    count, _, _, half, _ = half_ref.shape
    copies = []
    for p in range(count):
        start = (2 * p + (p + near) % 2) * half
        copies.append(pltpu.make_async_copy(half_ref.at[p], out_ref.at[:, :, pl.ds(start, half), :], sems.at[p]))
    for copy in copies:
        copy.start()
    for copy in copies:
        copy.wait()


def unpack_call(near, part, whole=None):
    count, held, levels, half, rows = part.shape
    anywhere = pl.BlockSpec(memory_space=pl.ANY)
    others = [] if whole is None else [whole]
    return pl.pallas_call(
        functools.partial(unpack_kernel, near),
        in_specs=[pl.BlockSpec(memory_space=pltpu.VMEM)] + [anywhere] * len(others),
        out_specs=anywhere,
        out_shape=jax.ShapeDtypeStruct((held, levels, 2 * count * half, rows), bf16),
        scratch_shapes=[pltpu.SemaphoreType.DMA((count,))],
        input_output_aliases={1: 0} if others else {},
        name="unpack",
    )(*on_chip(part), *others)


def swap_pairs(count, first):
    pairs = []
    for i in range(first, count - 1, 2):
        pairs += [(i, i + 1), (i + 1, i)]
    return pairs


def local(state, obs_index, obs_count, obs_value, obs_var, radius):
    n_x = lax.axis_size("mem")
    n_y = lax.axis_size("gy")
    held, levels, all_cols, rows = state.shape
    cols = all_cols // n_x
    members = held * n_x
    assert cols == 2 * BLK
    obs_slots = obs_index[0, 0]
    slots = obs_slots.shape[0]

    def swap_x(value, first):
        return lax.ppermute(value, "mem", swap_pairs(n_x, first))

    def swap_y(value, first):
        return lax.ppermute(value, "gy", swap_pairs(n_y, first))

    def swap_xy(value, first_x, first_y):
        pairs = [
            (sx * n_y + sy, dx * n_y + dy)
            for sx, dx in swap_pairs(n_x, first_x)
            for sy, dy in swap_pairs(n_y, first_y)
        ]
        return lax.ppermute(value, ("mem", "gy"), pairs)

    y_steps = [first for first in (0, 1) if swap_pairs(n_y, first)]

    live = jnp.arange(slots, dtype=jnp.int32) < obs_count[0, 0]
    weight = jnp.where(live, 1.0 / obs_var[0, 0], 0.0)
    col_pos = (obs_slots // rows % cols).astype(f32)
    row_pos = (obs_slots % rows).astype(f32)
    reach = jnp.broadcast_to(radius[0, 0].astype(f32), (slots,))
    blank = jnp.zeros((META - 5, slots), f32)
    meta = jnp.concatenate([jnp.stack([obs_value[0, 0], weight, col_pos, row_pos, reach]), blank], axis=0)
    meta_column = jnp.stack([meta] + [swap_y(meta, first) for first in y_steps])
    near_meta = swap_x(meta_column, 0)
    far_meta = swap_x(meta_column, 1)
    tile = lax.all_to_all(pack_call(state, n_x, cols), "mem", split_axis=0, concat_axis=0, tiled=True)
    tile, meta_column, near_meta = lax.optimization_barrier((tile, meta_column, near_meta))
    tile = tile.reshape(members, levels * cols, rows)

    own = gather_call(tile, obs_slots)
    column = [own] + [swap_y(own, step) for step in y_steps]
    near = [swap_x(own, 0)] + [swap_xy(own, 0, step) for step in y_steps]
    far_own = swap_x(own, 1)
    tile = turn_call(tile)

    def send_back(analysed):
        analysed = analysed.reshape(n_x, held, levels, BLK, rows)
        return lax.all_to_all(analysed, "mem", split_axis=0, concat_axis=0, tiled=True)

    analysed = analyse_call(False, tile, column, near, (meta_column, near_meta), levels, cols)
    first = send_back(analysed)
    far = [far_own] + [swap_y(far_own, step) for step in y_steps]
    analysed = analyse_call(True, tile, column, far, (meta_column, far_meta), levels, cols)
    second = send_back(analysed)
    whole = unpack_call(1, first)
    return unpack_call(0, second, whole)


def solution(mesh):
    in_specs = (
        P("mem", None, None, "gy"),
        P("mem", "gy", None),
        P("mem", "gy"),
        P("mem", "gy", None),
        P("mem", "gy", None),
        P("mem", "gy"),
    )
    out_specs = P("mem", None, None, "gy")
    return jax.shard_map(local, mesh=mesh, in_specs=in_specs, out_specs=out_specs, check_vma=False)
```
